32 devices in a mesh: row: 4 (over y, x), col: 8 (over z, core).
Axes of the slice: x: 2, y: 2, z: 4, core: 2. Of those that a mesh axis runs over, the one named last changes fastest.
Arguments:
- left_points: float32 [2048, 128], P(('row', 'col')), may hold values from -3.3 to 3.3
- right_points: float32 [2048, 128], P(('row', 'col')), may hold values from -3.3 to 3.3
- left_cotangent: bfloat16 [2048, 128], P(('row', 'col')), may hold values from -6 to 6
- right_coefficient: bfloat16 [2048, 128], P(('row', 'col')), may hold values from -6 to 6
Outputs:
- left_final: float32 [2048, 128], P(('row', 'col'))
- right_final: float32 [2048, 128], P(('row', 'col'))
- left_grad: float32 [2048, 128], P(('row', 'col'))
- right_grad: float32 [2048, 128], P(('row', 'col'))
The draws below stay inside these ranges and needn't reach their ends.
All inputs are finite; a program needn't handle non-finite values.
Results may differ from the reference program's by a relative error of at most 0.019.
Values may be sent and summed in bfloat16 or wider, within the bound.
No kernel may reach another device: no remote copies, remote signals or barrier semaphores. Data moves between devices by JAX's collectives and lax.ppermute only.
A program may use at most 64 MiB of HBM per device.

```python
import jax
import jax.numpy as jnp
from jax import lax

F = 128
R = 128
PTS_DEV = 64
STEPS = 2
N = 2048
N_ROW = 4
N_COL = 8


def cluster_centers(key):
    center_key = jax.random.fold_in(key, 7001)
    center_scale = 0.6
    centers = jax.random.truncated_normal(center_key, -3.0, 3.0, (N_ROW * N_COL, F), jnp.float32)
    return centers * center_scale


def point_noise(key, salt):
    noise_key = jax.random.fold_in(key, salt)
    noise_scale = (32.0 / F) ** 0.5
    noise = jax.random.truncated_normal(noise_key, -3.0, 3.0, (N, F), jnp.float32)
    return noise * noise_scale


def draw_left_points(key, part):
    centers = cluster_centers(key)
    shuffled = jax.random.permutation(jax.random.fold_in(key, 7004), N).astype(jnp.int32)
    partner = shuffled % (N_ROW * N_COL)
    return centers[partner] + point_noise(key, 7002)


def draw_right_points(key, part):
    centers = cluster_centers(key)
    position = jnp.arange(N, dtype=jnp.int32)
    device = position // PTS_DEV
    return centers[device] + point_noise(key, 7003)


def shard_levels(own_key, dims, shards, low, top_value):
    def one(dim, blocks):
        draws = jax.random.uniform(jax.random.fold_in(jax.random.fold_in(own_key, 6), dim), (blocks,), jnp.float32, low / len(shards), top_value / len(shards))
        return jnp.repeat(jnp.exp(draws), dims[dim] // blocks).reshape((-1,) + (1,) * (len(dims) - dim - 1))

    loudness = one(*shards[0])
    for cut in shards[1:]:
        loudness = loudness * one(*cut)
    return loudness


def scatter_about(own_key, extent, width, bound, split=(), kind=jnp.bfloat16):
    values = width * jax.random.normal(own_key, extent, jnp.float32)
    if split:
        values = values * shard_levels(own_key, extent, split, -0.22, 0.18)
    return jnp.clip(values, -bound, bound).astype(kind)


def setup_inputs(seed: int = 0) -> dict:
    seeds = jax.random.split(jax.random.key(seed), 5)
    left_points = draw_left_points(jax.random.fold_in(seeds[4], 71), 0)
    right_points = draw_right_points(jax.random.fold_in(seeds[4], 71), 0)
    left_cotangent = scatter_about(seeds[2], (N, R), 1.0, 6.0, ((0, 32),))
    right_coefficient = scatter_about(seeds[3], (N, R), 1.0, 6.0, ((0, 32),))
    return {"left_points": left_points, "right_points": right_points, "left_cotangent": left_cotangent, "right_coefficient": right_coefficient}


inverse_width = 0.03125
grad_scale = 0.0625
descent_rate = 0.3


def tile_terms(left_bf, left_panel, right_bf, right_panel):
    left_rows = left_bf.shape[0]
    block_rows = min(512, left_rows)
    block_count = left_rows // block_rows
    feature_width = left_bf.shape[1]
    right_wide = right_bf.astype(jnp.float32)
    right_norm = jnp.sum(right_wide * right_wide, axis=1)
    contract_last = (((1,), (1,)), ((), ()))

    def visit_block(carried, pieces):
        accumulated, column_sum = carried
        piece_feat, piece_panel = pieces
        piece_wide = piece_feat.astype(jnp.float32)
        left_norm = jnp.sum(piece_wide * piece_wide, axis=1)
        crossed = lax.dot_general(piece_feat, right_bf, contract_last, preferred_element_type=jnp.float32)
        distance = left_norm[:, None] + right_norm[None, :] - 2.0 * crossed
        kernel = jnp.exp(-inverse_width * distance).astype(jnp.bfloat16)
        weight = lax.dot_general(piece_panel, right_panel, contract_last, preferred_element_type=jnp.float32)
        product = (weight * kernel.astype(jnp.float32)).astype(jnp.bfloat16)
        product_wide = product.astype(jnp.float32)
        left_term = jnp.dot(product, right_bf, preferred_element_type=jnp.float32) - jnp.sum(product_wide, axis=1)[:, None] * piece_wide
        accumulated = accumulated + lax.dot_general(product, piece_feat, (((0,), (0,)), ((), ())), preferred_element_type=jnp.float32)
        column_sum = column_sum + jnp.sum(product_wide, axis=0)
        return (accumulated, column_sum), left_term

    initial = (jnp.zeros((right_bf.shape[0], feature_width), jnp.float32), jnp.zeros((right_bf.shape[0],), jnp.float32))
    pieces = (left_bf.reshape(block_count, block_rows, feature_width), left_panel.reshape(block_count, block_rows, left_panel.shape[1]))
    (accumulated, column_sum), left_terms = lax.scan(visit_block, initial, pieces)
    return left_terms.reshape(left_rows, feature_width), accumulated - column_sum[:, None] * right_wide


def reference(left_points, right_points, left_cotangent, right_coefficient):
    left_values = left_points
    right_values = right_points
    left_grad = jnp.zeros_like(left_points)
    right_grad = jnp.zeros_like(right_points)
    for step_index in range(STEPS):
        left_term, right_term = tile_terms(left_values.astype(jnp.bfloat16), left_cotangent, right_values.astype(jnp.bfloat16), right_coefficient)
        left_grad = left_term * grad_scale
        right_grad = right_term * grad_scale
        left_values = left_values - descent_rate * left_grad
        right_values = right_values - descent_rate * right_grad
    return left_values, right_values, left_grad, right_grad
```

```python
import functools
import math

import jax
import jax.numpy as jnp
from jax import lax
from jax.experimental import pallas as pl
from jax.experimental.pallas import tpu as pltpu
from jax.sharding import PartitionSpec as P

STEPS = 2


inverse_width = 0.03125
grad_scale = 0.0625
descent_rate = 0.3


f32 = jnp.float32
bf16 = jnp.bfloat16
exp2_scale = inverse_width * math.log2(math.e)
step_scale = descent_rate * grad_scale
LAST = (((1,), (1,)), ((), ()))
FIRST = (((0,), (0,)), ((), ()))
VMEM_BUDGET = 40 << 20


def tile_terms(left_bf, left_panel, right_bf, right_panel):
    left_rows = left_bf.shape[0]
    block_rows = min(512, left_rows)
    block_count = left_rows // block_rows
    feature_width = left_bf.shape[1]
    right_wide = right_bf.astype(jnp.float32)
    right_norm = jnp.sum(right_wide * right_wide, axis=1)
    contract_last = (((1,), (1,)), ((), ()))

    def visit_block(carried, pieces):
        accumulated, column_sum = carried
        piece_feat, piece_panel = pieces
        piece_wide = piece_feat.astype(jnp.float32)
        left_norm = jnp.sum(piece_wide * piece_wide, axis=1)
        crossed = lax.dot_general(
            piece_feat, right_bf, contract_last, preferred_element_type=jnp.float32
        )
        distance = left_norm[:, None] + right_norm[None, :] - 2.0 * crossed
        kernel = jnp.exp(-inverse_width * distance).astype(jnp.bfloat16)
        weight = lax.dot_general(
            piece_panel, right_panel, contract_last, preferred_element_type=jnp.float32
        )
        product = (weight * kernel.astype(jnp.float32)).astype(jnp.bfloat16)
        product_wide = product.astype(jnp.float32)
        left_term = (
            jnp.dot(product, right_bf, preferred_element_type=jnp.float32)
            - jnp.sum(product_wide, axis=1)[:, None] * piece_wide
        )
        accumulated = accumulated + lax.dot_general(
            product, piece_feat, (((0,), (0,)), ((), ())), preferred_element_type=jnp.float32
        )
        column_sum = column_sum + jnp.sum(product_wide, axis=0)
        return ((accumulated, column_sum), left_term)

    initial = (
        jnp.zeros((right_bf.shape[0], feature_width), jnp.float32),
        jnp.zeros((right_bf.shape[0],), jnp.float32),
    )
    pieces = (
        left_bf.reshape(block_count, block_rows, feature_width),
        left_panel.reshape(block_count, block_rows, left_panel.shape[1]),
    )
    (accumulated, column_sum), left_terms = lax.scan(visit_block, initial, pieces)
    return (
        left_terms.reshape(left_rows, feature_width),
        accumulated - column_sum[:, None] * right_wide,
    )


def partitioned_body(left_points, right_points, left_cotangent, right_coefficient):
    left_panel = lax.all_gather(left_cotangent, "col", axis=0, tiled=True)
    right_panel = lax.all_gather(right_coefficient, "row", axis=0, tiled=True)
    left_own = left_points
    right_own = right_points
    left_grad = jnp.zeros_like(left_points)
    right_grad = jnp.zeros_like(right_points)
    for step_index in range(STEPS):
        left_bf = lax.all_gather(left_own.astype(jnp.bfloat16), "col", axis=0, tiled=True)
        right_bf = lax.all_gather(right_own.astype(jnp.bfloat16), "row", axis=0, tiled=True)
        left_term, right_term = tile_terms(left_bf, left_panel, right_bf, right_panel)
        if step_index + 1 < STEPS:
            left_step = (
                lax.psum_scatter(left_term, "col", scatter_dimension=0, tiled=True) * grad_scale
            )
            right_step = (
                lax.psum_scatter(right_term, "row", scatter_dimension=0, tiled=True) * grad_scale
            )
            left_own = left_own - descent_rate * left_step
            right_own = right_own - descent_rate * right_step
        else:
            left_grad = (
                lax.psum_scatter(left_term, "col", scatter_dimension=0, tiled=True) * grad_scale
            )
            right_grad = (
                lax.psum_scatter(right_term, "row", scatter_dimension=0, tiled=True) * grad_scale
            )
            left_own = left_own - descent_rate * left_grad
            right_own = right_own - descent_rate * right_grad
    return (left_own, right_own, left_grad, right_grad)


def norm_row(wide):
    square = wide * wide
    high = square.astype(bf16)
    low = (square - high.astype(f32)).astype(bf16)
    ones = jnp.ones((8, wide.shape[1]), bf16)
    return lax.dot_general(ones, high, LAST, preferred_element_type=f32) + lax.dot_general(
        ones, low, LAST, preferred_element_type=f32
    )


def fill(near, side, points, panel, feat, panel_out, base):
    blocks, _, width = near.shape[1:]
    rows = blocks * points
    feat[pl.ds(base, rows), :width] = near[side, :, :points, :].reshape(rows, width)
    panel_out[pl.ds(base, rows), :] = near[side, :, points:, :].reshape(rows, width)


def first_step_kernel(
    points, tile, near, far, left, right, sent, own, left_aug, left_panel, right_aug, right_panel, left_norm, right_norm, product
):
    width = near.shape[3]
    half = near.shape[1] * points
    fill(near, 0, points, None, left_aug, left_panel, 0)
    fill(far, 0, points, None, left_aug, left_panel, half)
    fill(near, 1, points, None, right_aug, right_panel, 0)
    left_aug[:, width:] = jnp.ones((2 * half, width), bf16)
    right_aug[:, width:] = jnp.ones((half, width), bf16)
    left_wide = left_aug[:, :width].astype(f32)
    left_norm[...] = jnp.broadcast_to(
        exp2_scale * jnp.sum(left_wide * left_wide, axis=1, keepdims=True), left_norm.shape
    )
    right_norm[...] = exp2_scale * norm_row(right_aug[:, :width].astype(f32))
    step = min(tile, half, 256)

    def visit(index, _):
        rows = pl.ds(pl.multiple_of(index * tile, tile), tile)
        feat = left_aug[rows, :width]
        panel = left_panel[rows, :]
        norm = jnp.concatenate([left_norm[rows, :]] * (step // width), axis=1)
        for first in range(0, half, step):
            columns = pl.ds(first, step)
            crossed = lax.dot_general(feat, right_aug[columns, :width], LAST, preferred_element_type=f32)
            weight = lax.dot_general(panel, right_panel[columns, :], LAST, preferred_element_type=f32)
            kernel = jnp.exp2((2.0 * exp2_scale) * crossed - norm - right_norm[0:1, columns])
            product[rows, columns] = (weight * kernel).astype(bf16)
        both = jnp.dot(product[rows, :], right_aug[...], preferred_element_type=f32)
        term = both[:, :width] - both[:, width:] * feat.astype(f32)
        sent[rows, :] = term.astype(bf16)

        @pl.when(index == 0)
        def _():
            own[:points, :] = left[...] - step_scale * term[:points, :]

        return 0

    lax.fori_loop(0, 2 * half // tile, visit, 0)
    for first in range(0, half, step):
        columns = pl.ds(first, step)
        both = lax.dot_general(product[:, columns], left_aug[...], FIRST, preferred_element_type=f32)
        wide = right_aug[columns, :width].astype(f32)
        change = step_scale * (both[:, :width] - both[:, width:] * wide)
        sent[pl.ds(2 * half + first, step), :] = (wide - change).astype(bf16)
        if first == 0:
            own[points:, :] = right[...] - change[:points, :]


def own_term(feat, panel, others, other_panels):
    crossed = lax.dot_general(feat, others, LAST, preferred_element_type=f32)
    weight = lax.dot_general(panel, other_panels, LAST, preferred_element_type=f32)
    wide = feat.astype(f32)
    norm = jnp.sum(wide * wide, axis=1, keepdims=True)
    other_norm = norm_row(others.astype(f32))[0:1, :]
    kernel = jnp.exp2(exp2_scale * (2.0 * crossed - norm - other_norm))
    product = (weight * kernel).astype(bf16)
    total = jnp.sum(product.astype(f32), axis=1, keepdims=True)
    return jnp.dot(product, others, preferred_element_type=f32) - total * wide


def last_step_kernel(
    points, near, far, sent, came, own, left_out, right_out, left_grad, right_grad, others, panels
):
    width = near.shape[3]
    half = near.shape[1] * points

    def blocks(ref, side, kind):
        return ref[side, :, kind * points : (kind + 1) * points, :].reshape(half, width)

    left_new = own[:points, :] - step_scale * came[half : half + points, :].astype(f32)
    right_new = own[points:, :]
    others[:half, :] = sent[2 * half :, :]
    others[half:, :] = came[2 * half :, :]
    panels[:half, :] = blocks(near, 1, 1)
    panels[half:, :] = blocks(far, 1, 1)
    grad = grad_scale * own_term(left_new.astype(bf16), near[0, 0, points:, :], others[...], panels[...])
    left_grad[...] = grad
    left_out[...] = left_new - descent_rate * grad
    for place, mine, ref in ((0, 0, near), (half, half, far)):
        change = sent[place : place + half, :].astype(f32) + came[half - place : 2 * half - place, :].astype(f32)
        others[place : place + half, :] = (blocks(ref, 0, 0).astype(f32) - step_scale * change).astype(bf16)
    panels[:half, :] = blocks(near, 0, 1)
    panels[half:, :] = blocks(far, 0, 1)
    grad = grad_scale * own_term(right_new.astype(bf16), near[1, 0, points:, :], others[...], panels[...])
    right_grad[...] = grad
    right_out[...] = right_new - descent_rate * grad


def replicated_body(rows, cols, left_points, right_points, left_cotangent, right_coefficient):
    points, width = left_points.shape
    pairs = cols // 2
    blocks = rows * pairs
    half = blocks * points
    vmem = pl.BlockSpec(memory_space=pltpu.VMEM)
    params = pltpu.CompilerParams(vmem_limit_bytes=VMEM_BUDGET)

    def along_col(x, k):
        return lax.ppermute(x, "col", [(i, (i + 2 * k) % cols) for i in range(cols)])

    def along_row(x, k):
        return lax.ppermute(x, "row", [(i, (i + k) % rows) for i in range(rows)])

    def partner(x):
        return lax.ppermute(x, "col", [(i, i ^ 1) for i in range(cols)])

    packed = jnp.stack(
        [
            jnp.concatenate([left_points.astype(bf16), left_cotangent], axis=0),
            jnp.concatenate([right_points.astype(bf16), right_coefficient], axis=0),
        ]
    )
    column = jnp.concatenate([packed] + [along_col(packed, k) for k in range(1, pairs)], axis=1)
    near = jnp.concatenate([column] + [along_row(column, k) for k in range(1, rows)], axis=1)
    far = partner(near)
    near = near.reshape(2, blocks, 2 * points, width)
    far = far.reshape(2, blocks, 2 * points, width)
    tile = math.gcd(512, 2 * half)
    sent, own = pl.pallas_call(
        functools.partial(first_step_kernel, points, tile),
        out_shape=(
            jax.ShapeDtypeStruct((3 * half, width), bf16),
            jax.ShapeDtypeStruct((2 * points, width), f32),
        ),
        in_specs=[vmem] * 4,
        out_specs=(vmem, vmem),
        scratch_shapes=[
            pltpu.VMEM((2 * half, 2 * width), bf16),
            pltpu.VMEM((2 * half, width), bf16),
            pltpu.VMEM((half, 2 * width), bf16),
            pltpu.VMEM((half, width), bf16),
            pltpu.VMEM((2 * half, width), f32),
            pltpu.VMEM((8, half), f32),
            pltpu.VMEM((2 * half, half), bf16),
        ],
        compiler_params=params,
    )(near, far, left_points, right_points)
    came = partner(sent)
    shape = jax.ShapeDtypeStruct((points, width), f32)
    return pl.pallas_call(
        functools.partial(last_step_kernel, points),
        out_shape=(shape,) * 4,
        in_specs=[vmem] * 5,
        out_specs=(vmem,) * 4,
        scratch_shapes=[pltpu.VMEM((2 * half, width), bf16)] * 2,
        compiler_params=params,
    )(near, far, sent, came, own)


def body(rows, cols, *arrays):
    points, width = arrays[0].shape
    total = rows * cols * points
    held = total * total + 16 * total * width
    same = all(x.shape == (points, width) for x in arrays)
    if STEPS == 2 and same and cols % 2 == 0 and width % 128 == 0 and held <= VMEM_BUDGET // 2:
        return replicated_body(rows, cols, *arrays)
    return partitioned_body(*arrays)


def solution(mesh):
    spec = P(("row", "col"), None)
    run = functools.partial(body, mesh.shape["row"], mesh.shape["col"])
    return jax.shard_map(run, mesh=mesh, in_specs=(spec,) * 4, out_specs=(spec,) * 4, check_vma=False)
```

```python
import functools
import math

import jax
import jax.numpy as jnp
from jax import lax
from jax.experimental import pallas as pl
from jax.experimental.pallas import tpu as pltpu
from jax.sharding import PartitionSpec as P


STEPS = 2


inverse_width = 0.03125
grad_scale = 0.0625
descent_rate = 0.3


f32 = jnp.float32
bf16 = jnp.bfloat16
exp2_scale = inverse_width * math.log2(math.e)
step_scale = descent_rate * grad_scale
LAST = (((1,), (1,)), ((), ()))
FIRST = (((0,), (0,)), ((), ()))
VMEM_BUDGET = 40 << 20


def tile_terms(left_bf, left_panel, right_bf, right_panel):
    left_rows = left_bf.shape[0]
    block_rows = min(512, left_rows)
    block_count = left_rows // block_rows
    feature_width = left_bf.shape[1]
    right_wide = right_bf.astype(jnp.float32)
    right_norm = jnp.sum(right_wide * right_wide, axis=1)
    contract_last = (((1,), (1,)), ((), ()))

    def visit_block(carried, pieces):
        accumulated, column_sum = carried
        piece_feat, piece_panel = pieces
        piece_wide = piece_feat.astype(jnp.float32)
        left_norm = jnp.sum(piece_wide * piece_wide, axis=1)
        crossed = lax.dot_general(
            piece_feat, right_bf, contract_last, preferred_element_type=jnp.float32
        )
        distance = left_norm[:, None] + right_norm[None, :] - 2.0 * crossed
        kernel = jnp.exp(-inverse_width * distance).astype(jnp.bfloat16)
        weight = lax.dot_general(
            piece_panel, right_panel, contract_last, preferred_element_type=jnp.float32
        )
        product = (weight * kernel.astype(jnp.float32)).astype(jnp.bfloat16)
        product_wide = product.astype(jnp.float32)
        left_term = (
            jnp.dot(product, right_bf, preferred_element_type=jnp.float32)
            - jnp.sum(product_wide, axis=1)[:, None] * piece_wide
        )
        accumulated = accumulated + lax.dot_general(
            product, piece_feat, (((0,), (0,)), ((), ())), preferred_element_type=jnp.float32
        )
        column_sum = column_sum + jnp.sum(product_wide, axis=0)
        return ((accumulated, column_sum), left_term)

    initial = (
        jnp.zeros((right_bf.shape[0], feature_width), jnp.float32),
        jnp.zeros((right_bf.shape[0],), jnp.float32),
    )
    pieces = (
        left_bf.reshape(block_count, block_rows, feature_width),
        left_panel.reshape(block_count, block_rows, left_panel.shape[1]),
    )
    (accumulated, column_sum), left_terms = lax.scan(visit_block, initial, pieces)
    return (
        left_terms.reshape(left_rows, feature_width),
        accumulated - column_sum[:, None] * right_wide,
    )


def partitioned_body(left_points, right_points, left_cotangent, right_coefficient):
    left_panel = lax.all_gather(left_cotangent, "col", axis=0, tiled=True)
    right_panel = lax.all_gather(right_coefficient, "row", axis=0, tiled=True)
    left_own = left_points
    right_own = right_points
    left_grad = jnp.zeros_like(left_points)
    right_grad = jnp.zeros_like(right_points)
    for step_index in range(STEPS):
        left_bf = lax.all_gather(left_own.astype(jnp.bfloat16), "col", axis=0, tiled=True)
        right_bf = lax.all_gather(right_own.astype(jnp.bfloat16), "row", axis=0, tiled=True)
        left_term, right_term = tile_terms(left_bf, left_panel, right_bf, right_panel)
        if step_index + 1 < STEPS:
            left_step = (
                lax.psum_scatter(left_term, "col", scatter_dimension=0, tiled=True) * grad_scale
            )
            right_step = (
                lax.psum_scatter(right_term, "row", scatter_dimension=0, tiled=True) * grad_scale
            )
            left_own = left_own - descent_rate * left_step
            right_own = right_own - descent_rate * right_step
        else:
            left_grad = (
                lax.psum_scatter(left_term, "col", scatter_dimension=0, tiled=True) * grad_scale
            )
            right_grad = (
                lax.psum_scatter(right_term, "row", scatter_dimension=0, tiled=True) * grad_scale
            )
            left_own = left_own - descent_rate * left_grad
            right_own = right_own - descent_rate * right_grad
    return (left_own, right_own, left_grad, right_grad)


def squares(wide):
    square = wide * wide
    high = square.astype(bf16)
    return jnp.concatenate([high, (square - high.astype(f32)).astype(bf16)], axis=1)


def norm_row(feat):
    both = squares(feat.astype(f32))
    return lax.dot_general(jnp.ones((8, both.shape[1]), bf16), both, LAST, preferred_element_type=f32)


def norm_column(feat):
    both = squares(feat.astype(f32))
    return jnp.dot(both, jnp.ones((both.shape[1], feat.shape[1]), bf16), preferred_element_type=f32)


def with_ones(feat):
    return jnp.concatenate([feat, jnp.ones_like(feat)], axis=1)


def rows_of(ref, side, kind):
    blocks, both, width = ref.shape[1:]
    points = both // 2
    return ref[side, :, kind * points : (kind + 1) * points, :].reshape(blocks * points, width)


def ones_rows(blocks, sets, side):
    return jnp.concatenate([with_ones(rows_of(blocks[x], side, 0)) for x in sets], axis=0)


def products(blocks, lefts, rights, place, left_norm, right_norm, product):
    size, width = left_norm.shape[1:]
    for m, left in enumerate(lefts):
        feat, panel = rows_of(blocks[left], 0, 0), rows_of(blocks[left], 0, 1)
        norm = jnp.concatenate([left_norm[place(left)]] * (size // width), axis=1)
        for n, k in enumerate(rights):
            crossed = lax.dot_general(feat, rows_of(blocks[k, 0], 1, 0), LAST, preferred_element_type=f32)
            weight = lax.dot_general(panel, rows_of(blocks[k, 0], 1, 1), LAST, preferred_element_type=f32)
            kernel = jnp.exp2((2.0 * exp2_scale) * crossed - norm - right_norm[k, 0:1, :])
            product[m * size : (m + 1) * size, n * size : (n + 1) * size] = (weight * kernel).astype(bf16)


def stage_kernel(plan, sets, *refs):
    rects, new_left, new_right, fresh_left, fresh_right, first = plan
    count = len(sets)
    blocks = dict(zip(sets, refs[:count]))
    state = refs[count + (0 if first else 4) : -1]
    left_sum, right_sum, left_norm, right_norm = state
    product = refs[-1]
    fresh_left, fresh_right = set(fresh_left), set(fresh_right)

    def place(left):
        return left[1] * (left_sum.shape[0] // 2) + left[0]

    for left in new_left:
        left_norm[place(left)] = exp2_scale * norm_column(rows_of(blocks[left], 0, 0))
    for k in new_right:
        right_norm[k] = exp2_scale * norm_row(rows_of(blocks[k, 0], 1, 0))
    for lefts, rights in rects:
        products(blocks, lefts, rights, place, left_norm, right_norm, product)
        others = ones_rows(blocks, [(k, 0) for k in rights], 1)
        size = others.shape[0] // len(rights)
        for m, left in enumerate(lefts):
            term = jnp.dot(
                product[m * size : (m + 1) * size, : len(rights) * size], others, preferred_element_type=f32
            )
            if left in fresh_left:
                fresh_left.discard(left)
                left_sum[place(left)] = term
            else:
                left_sum[place(left)] += term
        others = ones_rows(blocks, lefts, 0)
        for n, k in enumerate(rights):
            term = lax.dot_general(
                product[: len(lefts) * size, n * size : (n + 1) * size], others, FIRST, preferred_element_type=f32
            )
            if k in fresh_right:
                fresh_right.discard(k)
                right_sum[k] = term
            else:
                right_sum[k] += term


def left_kernel(rows, points_left, left_sum, right_norm, *refs):
    every, (sent, own, product, left_norm) = refs[: 2 * rows], refs[2 * rows :]
    blocks = {(i % rows, i // rows): x for i, x in enumerate(every)}
    last = (rows - 1, 1)
    size, width = left_sum.shape[1], left_sum.shape[2] // 2
    rights = list(range(rows))
    left_norm[0] = exp2_scale * norm_column(rows_of(blocks[last], 0, 0))
    products(blocks, [last], rights, lambda _: 0, left_norm, right_norm, product)
    for index in range(2 * rows):
        if index < 2 * rows - 1:
            both = left_sum[index]
        else:
            both = jnp.dot(product[...], ones_rows(blocks, [(k, 0) for k in rights], 1), preferred_element_type=f32)
        term = both[:, :width] - both[:, width:] * rows_of(every[index], 0, 0).astype(f32)
        sent[index * size : (index + 1) * size, :] = term.astype(bf16)
        if index == 0:
            own[...] = points_left[...] - step_scale * term[: own.shape[0], :]


def right_kernel(rows, points_right, right_sum, product, last, *refs):
    near, (sent, own) = refs[:rows], refs[rows:]
    size, width = right_sum.shape[1], right_sum.shape[2] // 2
    others = with_ones(rows_of(last, 0, 0))
    for index in range(rows):
        both = right_sum[index] + lax.dot_general(
            product[:, index * size : (index + 1) * size], others, FIRST, preferred_element_type=f32
        )
        wide = rows_of(near[index], 1, 0).astype(f32)
        change = step_scale * (both[:, :width] - both[:, width:] * wide)
        sent[index * size : (index + 1) * size, :] = (wide - change).astype(bf16)
        if index == 0:
            own[...] = points_right[...] - change[: own.shape[0], :]


def own_weights_kernel(rows, *refs):
    every, (left_weight, right_weight) = refs[: 2 * rows], refs[2 * rows :]
    points = left_weight.shape[0]
    size = left_weight.shape[1] // (2 * rows)
    for side, out in ((0, left_weight), (1, right_weight)):
        panel = every[0][side, 0, points:, :]
        for index in range(2 * rows):
            out[:, index * size : (index + 1) * size] = lax.dot_general(
                panel, rows_of(every[index], 1 - side, 1), LAST, preferred_element_type=f32
            )


def own_term(feat, weight, others):
    crossed = lax.dot_general(feat, others, LAST, preferred_element_type=f32)
    wide = feat.astype(f32)
    norm = jnp.sum(wide * wide, axis=1, keepdims=True)
    other_norm = norm_row(others)[0:1, :]
    kernel = jnp.exp2(exp2_scale * (2.0 * crossed - norm - other_norm))
    product = (weight * kernel).astype(bf16)
    total = jnp.sum(product.astype(f32), axis=1, keepdims=True)
    return jnp.dot(product, others, preferred_element_type=f32) - total * wide


def last_right_kernel(rows, sent, came, own, weight, *refs):
    every, (new, grad, others) = refs[: 2 * rows], refs[2 * rows :]
    half = sent.shape[0] // 2
    size = half // rows
    for index in range(2 * rows):
        mine = index * size
        theirs = (mine + half) % (2 * half)
        change = sent[mine : mine + size, :].astype(f32) + came[theirs : theirs + size, :].astype(f32)
        feat = rows_of(every[index], 0, 0).astype(f32) - step_scale * change
        others[mine : mine + size, :] = feat.astype(bf16)
    value = own[...]
    term = grad_scale * own_term(value.astype(bf16), weight[...], others[...])
    grad[...] = term
    new[...] = value - descent_rate * term


def last_left_kernel(left_came, sent, came, own, weight, right_new, right_grad, *refs):
    outs, (others, new, grad, sems) = refs[:4], refs[4:]
    copies = [
        pltpu.make_async_copy(x, out, sems.at[i])
        for i, (x, out) in enumerate(zip((right_new, right_grad, new, grad), (outs[1], outs[3], outs[0], outs[2])))
    ]
    copies[0].start()
    copies[1].start()
    points = own.shape[0]
    half = sent.shape[0]
    others[:half, :] = sent[...]
    others[half:, :] = came[...]
    value = own[...] - step_scale * left_came[half : half + points, :].astype(f32)
    term = grad_scale * own_term(value.astype(bf16), weight[...], others[...])
    grad[...] = term
    new[...] = value - descent_rate * term
    copies[2].start()
    copies[3].start()
    for copy in copies:
        copy.wait()


def pack_kernel(left, right, left_panel, right_panel, out, left_held, right_held, sems):
    points = left.shape[0]
    moves = ((left, left_held), (right, right_held), (left_panel, out.at[0, points:]), (right_panel, out.at[1, points:]))
    copies = [pltpu.make_async_copy(source, target, sems.at[i]) for i, (source, target) in enumerate(moves)]
    for copy in copies:
        copy.start()
    for copy in copies:
        copy.wait()
    out[0, :points, :] = left_held[...].astype(bf16)
    out[1, :points, :] = right_held[...].astype(bf16)


def call(kernel, inputs, outputs, scratch=(), aliases=None, flops=0, in_space=pltpu.VMEM, out_space=pltpu.VMEM, limit=VMEM_BUDGET):
    moved = sum(x.size * x.dtype.itemsize for x in (*inputs, *outputs))
    return pl.pallas_call(
        kernel,
        out_shape=tuple(outputs),
        in_specs=[pl.BlockSpec(memory_space=in_space)] * len(inputs),
        out_specs=(pl.BlockSpec(memory_space=out_space),) * len(outputs),
        scratch_shapes=list(scratch),
        input_output_aliases=aliases or {},
        cost_estimate=pl.CostEstimate(flops=flops, bytes_accessed=moved // 8, transcendentals=0),
        compiler_params=pltpu.CompilerParams(vmem_limit_bytes=limit),
    )(*inputs)


def replicated_body(rows, cols, left_points, right_points, left_cotangent, right_coefficient):
    points, width = left_points.shape
    pairs = cols // 2
    size = pairs * points
    shape = jax.ShapeDtypeStruct

    def along_col(x, k):
        return lax.ppermute(x, "col", [(i, (i + 2 * k) % cols) for i in range(cols)])

    def along_row(x, k):
        def target(i):
            return i ^ k if rows & (rows - 1) == 0 else (i + k) % rows

        return lax.ppermute(x, "row", [(i, target(i)) for i in range(rows)])

    def partner(x):
        return lax.ppermute(x, "col", [(i, i ^ 1) for i in range(cols)])

    own_shape = shape((points, width), f32)
    packed, left_held, right_held = call(
        pack_kernel,
        [pltpu.with_memory_space_constraint(x, pltpu.HBM) for x in (left_points, right_points, left_cotangent, right_coefficient)],
        [shape((2, 2 * points, width), bf16), own_shape, own_shape],
        [pltpu.SemaphoreType.DMA((4,))],
        in_space=pl.ANY,
    )
    across = jnp.concatenate([along_col(packed, k) for k in range(1, pairs)], axis=1)
    direct = [packed] + [along_row(packed, k) for k in range(1, rows)]
    rest = [across] + [along_row(across, k) for k in range(1, rows)]
    blocks = {}
    for k in range(rows):
        near = jnp.concatenate([direct[k], rest[k]], axis=1)
        blocks[k, 0] = near.reshape(2, pairs, 2 * points, width)
        blocks[k, 1] = partner(near).reshape(2, pairs, 2 * points, width)

    state = (
        shape((2 * rows, size, 2 * width), f32),
        shape((rows, size, 2 * width), f32),
        shape((2 * rows, size, width), f32),
        shape((rows, 8, size), f32),
    )
    values = None
    seen_left, seen_right = set(), set()

    def stage(rects, new_left, new_right):
        nonlocal values
        sets = sorted({x for lefts, _ in rects for x in lefts} | {(k, 0) for _, rights in rects for k in rights})
        lefts = {x for part, _ in rects for x in part}
        rights = {k for _, part in rects for k in part}
        plan = (rects, new_left, new_right, lefts - seen_left, rights - seen_right, values is None)
        seen_left.update(lefts)
        seen_right.update(rights)
        inputs = [blocks[x] for x in sets] + list(values or ())
        values = call(
            functools.partial(stage_kernel, plan, sets),
            inputs,
            state,
            [pltpu.VMEM((max(len(a) for a, _ in rects) * size, max(len(b) for _, b in rects) * size), bf16)],
            aliases={len(sets) + i: i for i in range(4)} if values else None,
            flops=sum(len(a) * len(b) for a, b in rects) * 12 * size * size * width,
        )

    waiting = []
    for k in range(rows):
        old = [(i, half) for half in (0, 1) for i in range(k) if (i, half) in seen_left]
        rects = ([(old, [k])] if old else []) + [([(k, 0)], list(range(k + 1)))]
        stage(rects, [(k, 0)], [k])
        waiting.append((k, 1))
        if k != 1 and k != rows - 1:
            stage([(waiting, list(range(k + 1)))], waiting, [])
            waiting = []
    if waiting[:-1]:
        stage([(waiting[:-1], list(range(rows)))], waiting[:-1], [])
    left_sum, right_sum, _, right_norm = values
    near = [blocks[k, 0] for k in range(rows)]
    every = near + [blocks[k, 1] for k in range(rows)]
    left_sent, left_own, product = call(
        functools.partial(left_kernel, rows),
        [left_held, left_sum, right_norm] + every,
        [shape((2 * rows * size, width), bf16), own_shape, shape((size, rows * size), bf16)],
        [pltpu.VMEM((1, size, width), f32)],
    )
    left_came = partner(left_sent)
    right_sent, right_own = call(
        functools.partial(right_kernel, rows),
        [right_held, right_sum, product, blocks[rows - 1, 1]] + near,
        [shape((rows * size, width), bf16), own_shape],
    )
    right_came = partner(right_sent)
    left_weight, right_weight = call(
        functools.partial(own_weights_kernel, rows), every, [shape((points, 2 * rows * size), f32)] * 2
    )
    scratch = [pltpu.VMEM((2 * rows * size, width), bf16)]
    right_new, right_grad = call(
        functools.partial(last_right_kernel, rows),
        [left_sent, left_came, right_own, right_weight] + every,
        [own_shape] * 2,
        scratch,
    )
    return call(
        last_left_kernel,
        [left_came, right_sent, right_came, left_own, left_weight, right_new, right_grad],
        [own_shape] * 4,
        scratch + [pltpu.VMEM((points, width), f32)] * 2 + [pltpu.SemaphoreType.DMA((4,))],
        out_space=pltpu.HBM,
    )


def replicated(rows, cols, shapes):
    points, width = shapes[0]
    total = rows * cols * points
    held = total * total + 24 * total * width
    size = cols // 2 * points
    even = cols % 2 == 0 and width % 128 == 0 and size % width == 0 and rows > 2 and cols > 2
    return STEPS == 2 and even and len(set(shapes)) == 1 and held <= VMEM_BUDGET // 2


def body(rows, cols, *arrays):
    if replicated(rows, cols, [x.shape for x in arrays]):
        return replicated_body(rows, cols, *arrays)
    return partitioned_body(*arrays)


def solution(mesh):
    spec = P(("row", "col"), None)
    rows, cols = mesh.shape["row"], mesh.shape["col"]
    run = functools.partial(body, rows, cols)
    return jax.shard_map(run, mesh=mesh, in_specs=(spec,) * 4, out_specs=(spec,) * 4, check_vma=False)
```

```python
import functools
import math

import jax
import jax.numpy as jnp
from jax import lax
from jax.experimental import pallas as pl
from jax.experimental.pallas import tpu as pltpu
from jax.sharding import PartitionSpec as P


STEPS = 2


inverse_width = 0.03125
grad_scale = 0.0625
descent_rate = 0.3


f32 = jnp.float32
bf16 = jnp.bfloat16
exp2_scale = inverse_width * math.log2(math.e)
step_scale = descent_rate * grad_scale
LAST = (((1,), (1,)), ((), ()))
FIRST = (((0,), (0,)), ((), ()))
VMEM_BUDGET = 40 << 20


def tile_terms(left_bf, left_panel, right_bf, right_panel):
    left_rows = left_bf.shape[0]
    block_rows = min(512, left_rows)
    block_count = left_rows // block_rows
    feature_width = left_bf.shape[1]
    right_wide = right_bf.astype(jnp.float32)
    right_norm = jnp.sum(right_wide * right_wide, axis=1)
    contract_last = (((1,), (1,)), ((), ()))

    def visit_block(carried, pieces):
        accumulated, column_sum = carried
        piece_feat, piece_panel = pieces
        piece_wide = piece_feat.astype(jnp.float32)
        left_norm = jnp.sum(piece_wide * piece_wide, axis=1)
        crossed = lax.dot_general(
            piece_feat, right_bf, contract_last, preferred_element_type=jnp.float32
        )
        distance = left_norm[:, None] + right_norm[None, :] - 2.0 * crossed
        kernel = jnp.exp(-inverse_width * distance).astype(jnp.bfloat16)
        weight = lax.dot_general(
            piece_panel, right_panel, contract_last, preferred_element_type=jnp.float32
        )
        product = (weight * kernel.astype(jnp.float32)).astype(jnp.bfloat16)
        product_wide = product.astype(jnp.float32)
        left_term = (
            jnp.dot(product, right_bf, preferred_element_type=jnp.float32)
            - jnp.sum(product_wide, axis=1)[:, None] * piece_wide
        )
        accumulated = accumulated + lax.dot_general(
            product, piece_feat, (((0,), (0,)), ((), ())), preferred_element_type=jnp.float32
        )
        column_sum = column_sum + jnp.sum(product_wide, axis=0)
        return ((accumulated, column_sum), left_term)

    initial = (
        jnp.zeros((right_bf.shape[0], feature_width), jnp.float32),
        jnp.zeros((right_bf.shape[0],), jnp.float32),
    )
    pieces = (
        left_bf.reshape(block_count, block_rows, feature_width),
        left_panel.reshape(block_count, block_rows, left_panel.shape[1]),
    )
    (accumulated, column_sum), left_terms = lax.scan(visit_block, initial, pieces)
    return (
        left_terms.reshape(left_rows, feature_width),
        accumulated - column_sum[:, None] * right_wide,
    )


def partitioned_body(left_points, right_points, left_cotangent, right_coefficient):
    left_panel = lax.all_gather(left_cotangent, "col", axis=0, tiled=True)
    right_panel = lax.all_gather(right_coefficient, "row", axis=0, tiled=True)
    left_own = left_points
    right_own = right_points
    left_grad = jnp.zeros_like(left_points)
    right_grad = jnp.zeros_like(right_points)
    for step_index in range(STEPS):
        left_bf = lax.all_gather(left_own.astype(jnp.bfloat16), "col", axis=0, tiled=True)
        right_bf = lax.all_gather(right_own.astype(jnp.bfloat16), "row", axis=0, tiled=True)
        left_term, right_term = tile_terms(left_bf, left_panel, right_bf, right_panel)
        if step_index + 1 < STEPS:
            left_step = (
                lax.psum_scatter(left_term, "col", scatter_dimension=0, tiled=True) * grad_scale
            )
            right_step = (
                lax.psum_scatter(right_term, "row", scatter_dimension=0, tiled=True) * grad_scale
            )
            left_own = left_own - descent_rate * left_step
            right_own = right_own - descent_rate * right_step
        else:
            left_grad = (
                lax.psum_scatter(left_term, "col", scatter_dimension=0, tiled=True) * grad_scale
            )
            right_grad = (
                lax.psum_scatter(right_term, "row", scatter_dimension=0, tiled=True) * grad_scale
            )
            left_own = left_own - descent_rate * left_grad
            right_own = right_own - descent_rate * right_grad
    return (left_own, right_own, left_grad, right_grad)


def squares(wide):
    square = wide * wide
    high = square.astype(bf16)
    return jnp.concatenate([high, (square - high.astype(f32)).astype(bf16)], axis=1)


def norm_row(feat):
    both = squares(feat.astype(f32))
    return lax.dot_general(jnp.ones((8, both.shape[1]), bf16), both, LAST, preferred_element_type=f32)


def norm_column(feat):
    both = squares(feat.astype(f32))
    return jnp.dot(both, jnp.ones((both.shape[1], feat.shape[1]), bf16), preferred_element_type=f32)


def with_ones(feat):
    return jnp.concatenate([feat, jnp.ones_like(feat)], axis=1)


def rows_of(ref, side, kind):
    blocks, both, width = ref.shape[1:]
    points = both // 2
    return ref[side, :, kind * points : (kind + 1) * points, :].reshape(blocks * points, width)


def ones_rows(blocks, sets, side):
    return jnp.concatenate([with_ones(rows_of(blocks[x], side, 0)) for x in sets], axis=0)


def products(blocks, lefts, rights, place, left_norm, right_norm, product):
    size, width = left_norm.shape[1:]
    for m, left in enumerate(lefts):
        feat, panel = rows_of(blocks[left], 0, 0), rows_of(blocks[left], 0, 1)
        norm = jnp.concatenate([left_norm[place(left)]] * (size // width), axis=1)
        for n, k in enumerate(rights):
            crossed = lax.dot_general(feat, rows_of(blocks[k, 0], 1, 0), LAST, preferred_element_type=f32)
            weight = lax.dot_general(panel, rows_of(blocks[k, 0], 1, 1), LAST, preferred_element_type=f32)
            kernel = jnp.exp2((2.0 * exp2_scale) * crossed - norm - right_norm[k, 0:1, :])
            product[m * size : (m + 1) * size, n * size : (n + 1) * size] = (weight * kernel).astype(bf16)


def stage_kernel(plan, sets, *refs):
    rects, new_left, new_right, fresh_left, fresh_right, first, keep = plan
    count = len(sets)
    blocks = dict(zip(sets, refs[:count]))
    outs = refs[count + (0 if first else 4) :]
    left_sum, right_sum, left_norm, right_norm = outs[:4]
    fresh_left, fresh_right = set(fresh_left), set(fresh_right)

    def place(left):
        return left[1] * (left_sum.shape[0] // 2) + left[0]

    for left in new_left:
        left_norm[place(left)] = exp2_scale * norm_column(rows_of(blocks[left], 0, 0))
    for k in new_right:
        right_norm[k] = exp2_scale * norm_row(rows_of(blocks[k, 0], 1, 0))
    for index, (lefts, rights) in enumerate(rects):
        product = outs[4 + index] if keep else outs[4]
        products(blocks, lefts, rights, place, left_norm, right_norm, product)
        others = ones_rows(blocks, [(k, 0) for k in rights], 1)
        size = others.shape[0] // len(rights)
        for m, left in enumerate(lefts):
            term = jnp.dot(
                product[m * size : (m + 1) * size, : len(rights) * size], others, preferred_element_type=f32
            )
            if left in fresh_left:
                fresh_left.discard(left)
                left_sum[place(left)] = term
            else:
                left_sum[place(left)] += term
        if keep:
            continue
        others = ones_rows(blocks, lefts, 0)
        for n, k in enumerate(rights):
            term = lax.dot_general(
                product[: len(lefts) * size, n * size : (n + 1) * size], others, FIRST, preferred_element_type=f32
            )
            if k in fresh_right:
                fresh_right.discard(k)
                right_sum[k] = term
            else:
                right_sum[k] += term


def left_kernel(rows, points_left, left_sum, right_norm, *refs):
    every, (sent, base, own, product, left_norm) = refs[: 2 * rows], refs[2 * rows :]
    blocks = {(i % rows, i // rows): x for i, x in enumerate(every)}
    last = (rows - 1, 1)
    size, width = left_sum.shape[1], left_sum.shape[2] // 2
    rights = list(range(rows))
    left_norm[0] = exp2_scale * norm_column(rows_of(blocks[last], 0, 0))
    products(blocks, [last], rights, lambda _: 0, left_norm, right_norm, product)
    for index in range(2 * rows):
        if index < 2 * rows - 1:
            both = left_sum[index]
        else:
            both = jnp.dot(product[...], ones_rows(blocks, [(k, 0) for k in rights], 1), preferred_element_type=f32)
        wide = rows_of(every[index], 0, 0).astype(f32)
        change = step_scale * (both[:, :width] - both[:, width:] * wide)
        sent[index * size : (index + 1) * size, :] = change.astype(bf16)
        base[index * size : (index + 1) * size, :] = wide - change
        if index == 0:
            own[...] = points_left[...] - change[: own.shape[0], :]


def right_kernel(rows, summed, pieces, points_right, right_sum, *refs):
    kept, refs = refs[: len(pieces)], refs[len(pieces) :]
    every, (sent, norms, own) = refs[: 2 * rows], refs[2 * rows :]
    blocks = {(i % rows, i // rows): x for i, x in enumerate(every)}
    size, width = right_sum.shape[1], right_sum.shape[2] // 2
    for index in range(rows):
        terms = [right_sum[index]] if index in summed else []
        for (lefts, rights), product in zip(pieces, kept):
            if index in rights:
                n = rights.index(index)
                terms.append(
                    lax.dot_general(
                        product[:, n * size : (n + 1) * size],
                        ones_rows(blocks, lefts, 0),
                        FIRST,
                        preferred_element_type=f32,
                    )
                )
        both = sum(terms[1:], terms[0])
        wide = rows_of(every[index], 1, 0).astype(f32)
        change = step_scale * (both[:, :width] - both[:, width:] * wide)
        new = (wide - change).astype(bf16)
        sent[index * size : (index + 1) * size, :] = new
        norms[:, index * size : (index + 1) * size] = norm_row(new)
        if index == 0:
            own[...] = points_right[...] - change[: own.shape[0], :]


def own_weights_kernel(rows, sets, *refs):
    mine, every = refs[0], refs[1 : 1 + len(sets)]
    left_weight, right_weight = refs[-2:]
    points = left_weight.shape[0]
    size = left_weight.shape[1] // (2 * rows)
    for side, out in ((0, left_weight), (1, right_weight)):
        panel = mine[side, 0, points:, :]
        for (k, half), ref in zip(sets, every):
            index = half * rows + k
            out[:, index * size : (index + 1) * size] = lax.dot_general(
                panel, rows_of(ref, 1 - side, 1), LAST, preferred_element_type=f32
            )


def own_term(feat, weight, others, other_norm):
    crossed = lax.dot_general(feat, others, LAST, preferred_element_type=f32)
    wide = feat.astype(f32)
    norm = jnp.sum(wide * wide, axis=1, keepdims=True)
    kernel = jnp.exp2(exp2_scale * (2.0 * crossed - norm - other_norm))
    product = (weight * kernel).astype(bf16)
    total = jnp.sum(product.astype(f32), axis=1, keepdims=True)
    return jnp.dot(product, others, preferred_element_type=f32) - total * wide


def last_right_kernel(base, came, own, weight, new, grad):
    half = base.shape[0] // 2
    others = [
        (base[:half, :] - came[half:, :].astype(f32)).astype(bf16),
        (base[half:, :] - came[:half, :].astype(f32)).astype(bf16),
    ]
    value = own[...]
    norm = jnp.concatenate([norm_row(x)[0:1, :] for x in others], axis=1)
    others = jnp.concatenate(others, axis=0)
    term = grad_scale * own_term(value.astype(bf16), weight[...], others, norm)
    grad[...] = term
    new[...] = value - descent_rate * term


def last_left_kernel(left_came, sent, sent_norm, came, own, weight, right_new, right_grad, *refs):
    outs, (new, grad, sems) = refs[:4], refs[4:]
    copies = [
        pltpu.make_async_copy(x, out, sems.at[i])
        for i, (x, out) in enumerate(zip((right_new, right_grad, new, grad), (outs[1], outs[3], outs[0], outs[2])))
    ]
    copies[0].start()
    copies[1].start()
    points = own.shape[0]
    half = sent.shape[0]
    others = jnp.concatenate([sent[...], came[...]], axis=0)
    norm = jnp.concatenate([sent_norm[0:1, :], norm_row(came[...])[0:1, :]], axis=1)
    value = own[...] - left_came[half : half + points, :].astype(f32)
    term = grad_scale * own_term(value.astype(bf16), weight[...], others, norm)
    grad[...] = term
    new[...] = value - descent_rate * term
    copies[2].start()
    copies[3].start()
    for copy in copies:
        copy.wait()


def pack_kernel(left, right, left_panel, right_panel, out, left_held, right_held, sems):
    points = left.shape[0]
    moves = ((left, left_held), (right, right_held), (left_panel, out.at[0, points:]), (right_panel, out.at[1, points:]))
    copies = [pltpu.make_async_copy(source, target, sems.at[i]) for i, (source, target) in enumerate(moves)]
    for copy in copies:
        copy.start()
    for copy in copies:
        copy.wait()
    out[0, :points, :] = left_held[...].astype(bf16)
    out[1, :points, :] = right_held[...].astype(bf16)


def call(kernel, inputs, outputs, scratch=(), aliases=None, flops=0, in_space=pltpu.VMEM, out_space=pltpu.VMEM, limit=VMEM_BUDGET):
    moved = sum(x.size * x.dtype.itemsize for x in (*inputs, *outputs))
    return pl.pallas_call(
        kernel,
        out_shape=tuple(outputs),
        in_specs=[pl.BlockSpec(memory_space=in_space)] * len(inputs),
        out_specs=(pl.BlockSpec(memory_space=out_space),) * len(outputs),
        scratch_shapes=list(scratch),
        input_output_aliases=aliases or {},
        cost_estimate=pl.CostEstimate(flops=flops, bytes_accessed=moved // 8, transcendentals=0),
        compiler_params=pltpu.CompilerParams(vmem_limit_bytes=limit),
    )(*inputs)


def replicated_body(rows, cols, left_points, right_points, left_cotangent, right_coefficient):
    points, width = left_points.shape
    pairs = cols // 2
    size = pairs * points
    shape = jax.ShapeDtypeStruct

    def along_col(x, k):
        return lax.ppermute(x, "col", [(i, (i + 2 * k) % cols) for i in range(cols)])

    def along_row(x, k):
        def target(i):
            return i ^ k if rows & (rows - 1) == 0 else (i + k) % rows

        return lax.ppermute(x, "row", [(i, target(i)) for i in range(rows)])

    def partner(x):
        return lax.ppermute(x, "col", [(i, i ^ 1) for i in range(cols)])

    own_shape = shape((points, width), f32)
    packed, left_held, right_held = call(
        pack_kernel,
        [pltpu.with_memory_space_constraint(x, pltpu.HBM) for x in (left_points, right_points, left_cotangent, right_coefficient)],
        [shape((2, 2 * points, width), bf16), own_shape, own_shape],
        [pltpu.SemaphoreType.DMA((4,))],
        in_space=pl.ANY,
    )
    line = [along_col(packed, k) for k in range(1, pairs)]
    across = jnp.concatenate(line, axis=1)
    direct = [packed] + [along_row(packed, k) for k in range(1, rows)]
    rest = [across] + [along_row(across, k) for k in range(1, rows - 1)]
    own = jnp.concatenate([x for k, x in enumerate(line, 1) if k not in (1,)], axis=1)
    own = jnp.split(along_row(own, rows - 1), pairs - 1 - len((1,)), axis=1)
    parts = [along_col(direct[-1], k) if k in (1,) else own.pop(0) for k in range(1, pairs)]
    rest.append(jnp.concatenate(parts, axis=1))
    blocks = {}
    for k in range(rows):
        near = jnp.concatenate([direct[k], rest[k]], axis=1)
        blocks[k, 0] = near.reshape(2, pairs, 2 * points, width)
        blocks[k, 1] = partner(near).reshape(2, pairs, 2 * points, width)

    state = (
        shape((2 * rows, size, 2 * width), f32),
        shape((rows, size, 2 * width), f32),
        shape((2 * rows, size, width), f32),
        shape((rows, 8, size), f32),
    )
    values = None
    seen_left, seen_right = set(), set()

    def stage(rects, new_left, new_right, keep=False):
        nonlocal values
        sets = sorted({x for lefts, _ in rects for x in lefts} | {(k, 0) for _, rights in rects for k in rights})
        lefts = {x for part, _ in rects for x in part}
        rights = {k for _, part in rects for k in part}
        plan = (rects, new_left, new_right, lefts - seen_left, rights - seen_right, values is None, keep)
        seen_left.update(lefts)
        if not keep:
            seen_right.update(rights)
        places = [(len(a) * size, len(b) * size) for a, b in rects]
        inputs = [blocks[x] for x in sets] + list(values or ())
        values = call(
            functools.partial(stage_kernel, plan, sets),
            inputs,
            state + tuple(shape(x, bf16) for x in places if keep),
            [] if keep else [pltpu.VMEM(tuple(max(x) for x in zip(*places)), bf16)],
            aliases={len(sets) + i: i for i in range(4)} if values else None,
            flops=sum(len(a) * len(b) for a, b in rects) * 12 * size * size * width,
        )

    held = ()

    def weights(sets):
        return call(
            functools.partial(own_weights_kernel, rows, sets),
            [blocks[0, 0]] + [blocks[x] for x in sets] + list(held),
            [shape((points, 2 * rows * size), f32)] * 2,
            aliases={1 + len(sets) + i: i for i in range(2)} if held else None,
        )

    waiting = []
    for k in range(rows):
        if k == rows - 1:
            held = weights([(i, half) for half in (0, 1) for i in range(k)])
        old = [(i, half) for half in (0, 1) for i in range(k) if (i, half) in seen_left]
        rects = ([(old, [k])] if old else []) + [([(k, 0)], list(range(k + 1)))]
        stage(rects, [(k, 0)], [k], keep=k == rows - 1)
        if k == rows - 1:
            kept, values, pieces = values[4:], values[:4], rects
        waiting.append((k, 1))
        if k != 1 and k != rows - 1:
            stage([(waiting, list(range(k + 1)))], waiting, [])
            waiting = []
    if waiting[:-1]:
        more = [(waiting[:-1], list(range(rows)))]
        stage(more, waiting[:-1], [], keep=True)
        kept, values, pieces = [*kept, *values[4:]], values[:4], pieces + more
    left_sum, right_sum, _, right_norm = values
    near = [blocks[k, 0] for k in range(rows)]
    every = near + [blocks[k, 1] for k in range(rows)]
    left_sent, left_base, left_own, product = call(
        functools.partial(left_kernel, rows),
        [left_held, left_sum, right_norm] + every,
        [
            shape((2 * rows * size, width), bf16),
            shape((2 * rows * size, width), f32),
            own_shape,
            shape((size, rows * size), bf16),
        ],
        [pltpu.VMEM((1, size, width), f32)],
    )
    left_came = partner(left_sent)
    pieces = pieces + [([(rows - 1, 1)], list(range(rows)))]
    right_sent, right_row_norm, right_own = call(
        functools.partial(right_kernel, rows, seen_right, pieces),
        [right_held, right_sum, *kept, product] + every,
        [shape((rows * size, width), bf16), shape((8, rows * size), f32), own_shape],
    )
    right_came = partner(right_sent)
    left_weight, right_weight = weights([(rows - 1, 0), (rows - 1, 1)])
    right_new, right_grad = call(last_right_kernel, [left_base, left_came, right_own, right_weight], [own_shape] * 2)
    return call(
        last_left_kernel,
        [left_came, right_sent, right_row_norm, right_came, left_own, left_weight, right_new, right_grad],
        [own_shape] * 4,
        [pltpu.VMEM((points, width), f32)] * 2 + [pltpu.SemaphoreType.DMA((4,))],
        out_space=pltpu.HBM,
    )


def replicated(rows, cols, shapes):
    points, width = shapes[0]
    total = rows * cols * points
    held = total * total + 24 * total * width
    size = cols // 2 * points
    even = cols % 2 == 0 and width % 128 == 0 and size % width == 0 and rows > 2 and cols > 2
    return STEPS == 2 and even and len(set(shapes)) == 1 and held <= VMEM_BUDGET // 2


def body(rows, cols, *arrays):
    if replicated(rows, cols, [x.shape for x in arrays]):
        return replicated_body(rows, cols, *arrays)
    return partitioned_body(*arrays)


def solution(mesh):
    spec = P(("row", "col"), None)
    rows, cols = mesh.shape["row"], mesh.shape["col"]
    run = functools.partial(body, rows, cols)
    return jax.shard_map(run, mesh=mesh, in_specs=(spec,) * 4, out_specs=(spec,) * 4, check_vma=False)
```

```python
import functools
import math

import jax
import jax.numpy as jnp
from jax import lax
from jax.experimental import pallas as pl
from jax.experimental.pallas import tpu as pltpu
from jax.sharding import PartitionSpec as P


STEPS = 2


inverse_width = 0.03125
grad_scale = 0.0625
descent_rate = 0.3


f32 = jnp.float32
bf16 = jnp.bfloat16
exp2_scale = inverse_width * math.log2(math.e)
step_scale = descent_rate * grad_scale
LAST = (((1,), (1,)), ((), ()))
FIRST = (((0,), (0,)), ((), ()))
VMEM_BUDGET = 40 << 20


def tile_terms(left_bf, left_panel, right_bf, right_panel):
    left_rows = left_bf.shape[0]
    block_rows = min(512, left_rows)
    block_count = left_rows // block_rows
    feature_width = left_bf.shape[1]
    right_wide = right_bf.astype(jnp.float32)
    right_norm = jnp.sum(right_wide * right_wide, axis=1)
    contract_last = (((1,), (1,)), ((), ()))

    def visit_block(carried, pieces):
        accumulated, column_sum = carried
        piece_feat, piece_panel = pieces
        piece_wide = piece_feat.astype(jnp.float32)
        left_norm = jnp.sum(piece_wide * piece_wide, axis=1)
        crossed = lax.dot_general(
            piece_feat, right_bf, contract_last, preferred_element_type=jnp.float32
        )
        distance = left_norm[:, None] + right_norm[None, :] - 2.0 * crossed
        kernel = jnp.exp(-inverse_width * distance).astype(jnp.bfloat16)
        weight = lax.dot_general(
            piece_panel, right_panel, contract_last, preferred_element_type=jnp.float32
        )
        product = (weight * kernel.astype(jnp.float32)).astype(jnp.bfloat16)
        product_wide = product.astype(jnp.float32)
        left_term = (
            jnp.dot(product, right_bf, preferred_element_type=jnp.float32)
            - jnp.sum(product_wide, axis=1)[:, None] * piece_wide
        )
        accumulated = accumulated + lax.dot_general(
            product, piece_feat, (((0,), (0,)), ((), ())), preferred_element_type=jnp.float32
        )
        column_sum = column_sum + jnp.sum(product_wide, axis=0)
        return ((accumulated, column_sum), left_term)

    initial = (
        jnp.zeros((right_bf.shape[0], feature_width), jnp.float32),
        jnp.zeros((right_bf.shape[0],), jnp.float32),
    )
    pieces = (
        left_bf.reshape(block_count, block_rows, feature_width),
        left_panel.reshape(block_count, block_rows, left_panel.shape[1]),
    )
    (accumulated, column_sum), left_terms = lax.scan(visit_block, initial, pieces)
    return (
        left_terms.reshape(left_rows, feature_width),
        accumulated - column_sum[:, None] * right_wide,
    )


def partitioned_body(left_points, right_points, left_cotangent, right_coefficient):
    left_panel = lax.all_gather(left_cotangent, "col", axis=0, tiled=True)
    right_panel = lax.all_gather(right_coefficient, "row", axis=0, tiled=True)
    left_own = left_points
    right_own = right_points
    left_grad = jnp.zeros_like(left_points)
    right_grad = jnp.zeros_like(right_points)
    for step_index in range(STEPS):
        left_bf = lax.all_gather(left_own.astype(jnp.bfloat16), "col", axis=0, tiled=True)
        right_bf = lax.all_gather(right_own.astype(jnp.bfloat16), "row", axis=0, tiled=True)
        left_term, right_term = tile_terms(left_bf, left_panel, right_bf, right_panel)
        if step_index + 1 < STEPS:
            left_step = (
                lax.psum_scatter(left_term, "col", scatter_dimension=0, tiled=True) * grad_scale
            )
            right_step = (
                lax.psum_scatter(right_term, "row", scatter_dimension=0, tiled=True) * grad_scale
            )
            left_own = left_own - descent_rate * left_step
            right_own = right_own - descent_rate * right_step
        else:
            left_grad = (
                lax.psum_scatter(left_term, "col", scatter_dimension=0, tiled=True) * grad_scale
            )
            right_grad = (
                lax.psum_scatter(right_term, "row", scatter_dimension=0, tiled=True) * grad_scale
            )
            left_own = left_own - descent_rate * left_grad
            right_own = right_own - descent_rate * right_grad
    return (left_own, right_own, left_grad, right_grad)


def squares(wide):
    square = wide * wide
    high = square.astype(bf16)
    return jnp.concatenate([high, (square - high.astype(f32)).astype(bf16)], axis=1)


def norm_row(feat):
    both = squares(feat.astype(f32))
    return lax.dot_general(jnp.ones((8, both.shape[1]), bf16), both, LAST, preferred_element_type=f32)


def norm_column(feat):
    both = squares(feat.astype(f32))
    return jnp.dot(both, jnp.ones((both.shape[1], feat.shape[1]), bf16), preferred_element_type=f32)


def with_ones(feat):
    return jnp.concatenate([feat, jnp.ones_like(feat)], axis=1)


def rows_of(ref, side, kind):
    blocks, both, width = ref.shape[1:]
    points = both // 2
    return ref[side, :, kind * points : (kind + 1) * points, :].reshape(blocks * points, width)


def ones_rows(blocks, sets, side):
    return jnp.concatenate([with_ones(rows_of(blocks[x], side, 0)) for x in sets], axis=0)


def products(blocks, lefts, rights, place, left_norm, right_norm, product):
    size, width = left_norm.shape[1:]
    for m, left in enumerate(lefts):
        feat, panel = rows_of(blocks[left], 0, 0), rows_of(blocks[left], 0, 1)
        norm = jnp.concatenate([left_norm[place(left)]] * (size // width), axis=1)
        for n, k in enumerate(rights):
            crossed = lax.dot_general(feat, rows_of(blocks[k, 0], 1, 0), LAST, preferred_element_type=f32)
            weight = lax.dot_general(panel, rows_of(blocks[k, 0], 1, 1), LAST, preferred_element_type=f32)
            kernel = jnp.exp2((2.0 * exp2_scale) * crossed - norm - right_norm[k, 0:1, :])
            product[m * size : (m + 1) * size, n * size : (n + 1) * size] = (weight * kernel).astype(bf16)


def stage_kernel(plan, sets, *refs):
    rects, new_left, new_right, fresh_left, fresh_right, first, keep = plan
    count = len(sets)
    blocks = dict(zip(sets, refs[:count]))
    outs = refs[count + (0 if first else 4) :]
    left_sum, right_sum, left_norm, right_norm = outs[:4]
    fresh_left, fresh_right = set(fresh_left), set(fresh_right)

    def place(left):
        return left[1] * (left_sum.shape[0] // 2) + left[0]

    for left in new_left:
        left_norm[place(left)] = exp2_scale * norm_column(rows_of(blocks[left], 0, 0))
    for k in new_right:
        right_norm[k] = exp2_scale * norm_row(rows_of(blocks[k, 0], 1, 0))
    for index, (lefts, rights) in enumerate(rects):
        product = outs[4 + index] if keep else outs[4]
        products(blocks, lefts, rights, place, left_norm, right_norm, product)
        others = ones_rows(blocks, [(k, 0) for k in rights], 1)
        size = others.shape[0] // len(rights)
        for m, left in enumerate(lefts):
            term = jnp.dot(
                product[m * size : (m + 1) * size, : len(rights) * size], others, preferred_element_type=f32
            )
            if left in fresh_left:
                fresh_left.discard(left)
                left_sum[place(left)] = term
            else:
                left_sum[place(left)] += term
        if keep:
            continue
        others = ones_rows(blocks, lefts, 0)
        for n, k in enumerate(rights):
            term = lax.dot_general(
                product[: len(lefts) * size, n * size : (n + 1) * size], others, FIRST, preferred_element_type=f32
            )
            if k in fresh_right:
                fresh_right.discard(k)
                right_sum[k] = term
            else:
                right_sum[k] += term


def left_kernel(rows, points_left, left_sum, right_norm, *refs):
    every, (sent, base, own, product, left_norm) = refs[: 2 * rows], refs[2 * rows :]
    blocks = {(i % rows, i // rows): x for i, x in enumerate(every)}
    last = (rows - 1, 1)
    size, width = left_sum.shape[1], left_sum.shape[2] // 2
    rights = list(range(rows))
    left_norm[0] = exp2_scale * norm_column(rows_of(blocks[last], 0, 0))
    products(blocks, [last], rights, lambda _: 0, left_norm, right_norm, product)
    for index in range(2 * rows):
        if index < 2 * rows - 1:
            both = left_sum[index]
        else:
            both = jnp.dot(product[...], ones_rows(blocks, [(k, 0) for k in rights], 1), preferred_element_type=f32)
        wide = rows_of(every[index], 0, 0).astype(f32)
        change = step_scale * (both[:, :width] - both[:, width:] * wide)
        sent[index * size : (index + 1) * size, :] = change.astype(bf16)
        base[index * size : (index + 1) * size, :] = wide - change
        if index == 0:
            own[...] = points_left[...] - change[: own.shape[0], :]


def right_kernel(rows, summed, pieces, points_right, right_sum, *refs):
    kept, refs = refs[: len(pieces)], refs[len(pieces) :]
    every, (sent, norms, own) = refs[: 2 * rows], refs[2 * rows :]
    blocks = {(i % rows, i // rows): x for i, x in enumerate(every)}
    size, width = right_sum.shape[1], right_sum.shape[2] // 2
    for index in range(rows):
        terms = [right_sum[index]] if index in summed else []
        for (lefts, rights), product in zip(pieces, kept):
            if index in rights:
                n = rights.index(index)
                terms.append(
                    lax.dot_general(
                        product[:, n * size : (n + 1) * size],
                        ones_rows(blocks, lefts, 0),
                        FIRST,
                        preferred_element_type=f32,
                    )
                )
        both = sum(terms[1:], terms[0])
        wide = rows_of(every[index], 1, 0).astype(f32)
        change = step_scale * (both[:, :width] - both[:, width:] * wide)
        new = (wide - change).astype(bf16)
        sent[index * size : (index + 1) * size, :] = new
        norms[:, index * size : (index + 1) * size] = norm_row(new)
        if index == 0:
            own[...] = points_right[...] - change[: own.shape[0], :]


def own_weights_kernel(rows, sets, *refs):
    mine, every = refs[0], refs[1 : 1 + len(sets)]
    left_weight, right_weight = refs[-2:]
    points = left_weight.shape[0]
    size = left_weight.shape[1] // (2 * rows)
    for side, out in ((0, left_weight), (1, right_weight)):
        panel = mine[side, 0, points:, :]
        for (k, half), ref in zip(sets, every):
            index = half * rows + k
            out[:, index * size : (index + 1) * size] = lax.dot_general(
                panel, rows_of(ref, 1 - side, 1), LAST, preferred_element_type=f32
            )


def own_term(feat, weight, others, other_norm):
    crossed = lax.dot_general(feat, others, LAST, preferred_element_type=f32)
    wide = feat.astype(f32)
    norm = jnp.sum(wide * wide, axis=1, keepdims=True)
    kernel = jnp.exp2(exp2_scale * (2.0 * crossed - norm - other_norm))
    product = (weight * kernel).astype(bf16)
    total = jnp.sum(product.astype(f32), axis=1, keepdims=True)
    return jnp.dot(product, others, preferred_element_type=f32) - total * wide


def last_right_kernel(base, came, sent, sent_norm, own_right, own_left, right_weight, left_weight, *outs):
    new, grad, left_value, left_term = outs
    half, points = sent.shape[0], own_left.shape[0]
    left = own_left[...] - came[half : half + points, :].astype(f32)
    left_value[...] = left
    left_term[...] = own_term(left.astype(bf16), left_weight[:, :half], sent[...], sent_norm[0:1, :])
    others = [
        (base[:half, :] - came[half:, :].astype(f32)).astype(bf16),
        (base[half:, :] - came[:half, :].astype(f32)).astype(bf16),
    ]
    norm = jnp.concatenate([norm_row(x)[0:1, :] for x in others], axis=1)
    others = jnp.concatenate(others, axis=0)
    value = own_right[...]
    term = grad_scale * own_term(value.astype(bf16), right_weight[...], others, norm)
    grad[...] = term
    new[...] = value - descent_rate * term


def last_left_kernel(came, left_value, left_term, weight, right_new, right_grad, *refs):
    outs, (new, grad, sems) = refs[:4], refs[4:]
    copies = [
        pltpu.make_async_copy(x, out, sems.at[i])
        for i, (x, out) in enumerate(zip((right_new, right_grad, new, grad), (outs[1], outs[3], outs[0], outs[2])))
    ]
    copies[0].start()
    copies[1].start()
    half = came.shape[0]
    value = left_value[...]
    others = came[...]
    term = left_term[...] + own_term(value.astype(bf16), weight[:, half:], others, norm_row(others)[0:1, :])
    term = grad_scale * term
    grad[...] = term
    new[...] = value - descent_rate * term
    copies[2].start()
    copies[3].start()
    for copy in copies:
        copy.wait()


def pack_kernel(left, right, left_panel, right_panel, out, left_held, right_held, sems):
    points = left.shape[0]
    moves = ((left, left_held), (right, right_held), (left_panel, out.at[0, points:]), (right_panel, out.at[1, points:]))
    copies = [pltpu.make_async_copy(source, target, sems.at[i]) for i, (source, target) in enumerate(moves)]
    for copy in copies:
        copy.start()
    for copy in copies:
        copy.wait()
    out[0, :points, :] = left_held[...].astype(bf16)
    out[1, :points, :] = right_held[...].astype(bf16)


def call(kernel, inputs, outputs, scratch=(), aliases=None, flops=0, in_space=pltpu.VMEM, out_space=pltpu.VMEM, limit=VMEM_BUDGET):
    moved = sum(x.size * x.dtype.itemsize for x in (*inputs, *outputs))
    return pl.pallas_call(
        kernel,
        out_shape=tuple(outputs),
        in_specs=[pl.BlockSpec(memory_space=in_space)] * len(inputs),
        out_specs=(pl.BlockSpec(memory_space=out_space),) * len(outputs),
        scratch_shapes=list(scratch),
        input_output_aliases=aliases or {},
        cost_estimate=pl.CostEstimate(flops=flops, bytes_accessed=moved // 8, transcendentals=0),
        compiler_params=pltpu.CompilerParams(vmem_limit_bytes=limit),
    )(*inputs)


def replicated_body(rows, cols, left_points, right_points, left_cotangent, right_coefficient):
    points, width = left_points.shape
    pairs = cols // 2
    size = pairs * points
    shape = jax.ShapeDtypeStruct

    def along_col(x, k):
        return lax.ppermute(x, "col", [(i, (i + 2 * k) % cols) for i in range(cols)])

    def along_row(x, k):
        def target(i):
            return i ^ k if rows & (rows - 1) == 0 else (i + k) % rows

        return lax.ppermute(x, "row", [(i, target(i)) for i in range(rows)])

    def partner(x):
        return lax.ppermute(x, "col", [(i, i ^ 1) for i in range(cols)])

    own_shape = shape((points, width), f32)
    packed, left_held, right_held = call(
        pack_kernel,
        [pltpu.with_memory_space_constraint(x, pltpu.HBM) for x in (left_points, right_points, left_cotangent, right_coefficient)],
        [shape((2, 2 * points, width), bf16), own_shape, own_shape],
        [pltpu.SemaphoreType.DMA((4,))],
        in_space=pl.ANY,
    )
    line = [along_col(packed, k) for k in range(1, pairs)]
    across = jnp.concatenate(line, axis=1)
    direct = [packed] + [along_row(packed, k) for k in range(1, rows)]
    rest = [across] + [along_row(across, k) for k in range(1, rows - 1)]
    own = jnp.concatenate([x for k, x in enumerate(line, 1) if k not in (1,)], axis=1)
    own = jnp.split(along_row(own, rows - 1), pairs - 1 - len((1,)), axis=1)
    parts = [along_col(direct[-1], k) if k in (1,) else own.pop(0) for k in range(1, pairs)]
    rest.append(jnp.concatenate(parts, axis=1))
    blocks = {}
    for k in range(rows):
        near = jnp.concatenate([direct[k], rest[k]], axis=1)
        blocks[k, 0] = near.reshape(2, pairs, 2 * points, width)
        blocks[k, 1] = partner(near).reshape(2, pairs, 2 * points, width)

    state = (
        shape((2 * rows, size, 2 * width), f32),
        shape((rows, size, 2 * width), f32),
        shape((2 * rows, size, width), f32),
        shape((rows, 8, size), f32),
    )
    values = None
    seen_left, seen_right = set(), set()

    def stage(rects, new_left, new_right, keep=False):
        nonlocal values
        sets = sorted({x for lefts, _ in rects for x in lefts} | {(k, 0) for _, rights in rects for k in rights})
        lefts = {x for part, _ in rects for x in part}
        rights = {k for _, part in rects for k in part}
        plan = (rects, new_left, new_right, lefts - seen_left, rights - seen_right, values is None, keep)
        seen_left.update(lefts)
        if not keep:
            seen_right.update(rights)
        places = [(len(a) * size, len(b) * size) for a, b in rects]
        inputs = [blocks[x] for x in sets] + list(values or ())
        values = call(
            functools.partial(stage_kernel, plan, sets),
            inputs,
            state + tuple(shape(x, bf16) for x in places if keep),
            [] if keep else [pltpu.VMEM(tuple(max(x) for x in zip(*places)), bf16)],
            aliases={len(sets) + i: i for i in range(4)} if values else None,
            flops=sum(len(a) * len(b) for a, b in rects) * 12 * size * size * width,
        )

    held = ()

    def weights(sets):
        return call(
            functools.partial(own_weights_kernel, rows, sets),
            [blocks[0, 0]] + [blocks[x] for x in sets] + list(held),
            [shape((points, 2 * rows * size), f32)] * 2,
            aliases={1 + len(sets) + i: i for i in range(2)} if held else None,
        )

    waiting = []
    for k in range(rows):
        if k == rows - 1:
            held = weights([(i, half) for half in (0, 1) for i in range(k)])
        old = [(i, half) for half in (0, 1) for i in range(k) if (i, half) in seen_left]
        rects = ([(old, [k])] if old else []) + [([(k, 0)], list(range(k + 1)))]
        stage(rects, [(k, 0)], [k], keep=k == rows - 1)
        if k == rows - 1:
            kept, values, pieces = values[4:], values[:4], rects
        waiting.append((k, 1))
        if k != 1 and k != rows - 1:
            stage([(waiting, list(range(k + 1)))], waiting, [])
            waiting = []
    if waiting[:-1]:
        more = [(waiting[:-1], list(range(rows)))]
        stage(more, waiting[:-1], [], keep=True)
        kept, values, pieces = [*kept, *values[4:]], values[:4], pieces + more
    left_sum, right_sum, _, right_norm = values
    near = [blocks[k, 0] for k in range(rows)]
    every = near + [blocks[k, 1] for k in range(rows)]
    left_sent, left_base, left_own, product = call(
        functools.partial(left_kernel, rows),
        [left_held, left_sum, right_norm] + every,
        [
            shape((2 * rows * size, width), bf16),
            shape((2 * rows * size, width), f32),
            own_shape,
            shape((size, rows * size), bf16),
        ],
        [pltpu.VMEM((1, size, width), f32)],
    )
    left_came = partner(left_sent)
    pieces = pieces + [([(rows - 1, 1)], list(range(rows)))]
    right_sent, right_row_norm, right_own = call(
        functools.partial(right_kernel, rows, seen_right, pieces),
        [right_held, right_sum, *kept, product] + every,
        [shape((rows * size, width), bf16), shape((8, rows * size), f32), own_shape],
    )
    right_came = partner(right_sent)
    left_weight, right_weight = weights([(rows - 1, 0), (rows - 1, 1)])
    right_new, right_grad, left_value, left_term = call(
        last_right_kernel,
        [left_base, left_came, right_sent, right_row_norm, right_own, left_own, right_weight, left_weight],
        [own_shape] * 4,
    )
    return call(
        last_left_kernel,
        [right_came, left_value, left_term, left_weight, right_new, right_grad],
        [own_shape] * 4,
        [pltpu.VMEM((points, width), f32)] * 2 + [pltpu.SemaphoreType.DMA((4,))],
        out_space=pltpu.HBM,
    )


def replicated(rows, cols, shapes):
    points, width = shapes[0]
    total = rows * cols * points
    held = total * total + 24 * total * width
    size = cols // 2 * points
    even = cols % 2 == 0 and width % 128 == 0 and size % width == 0 and rows > 2 and cols > 2
    return STEPS == 2 and even and len(set(shapes)) == 1 and held <= VMEM_BUDGET // 2


def body(rows, cols, *arrays):
    if replicated(rows, cols, [x.shape for x in arrays]):
        return replicated_body(rows, cols, *arrays)
    return partitioned_body(*arrays)


def solution(mesh):
    spec = P(("row", "col"), None)
    rows, cols = mesh.shape["row"], mesh.shape["col"]
    run = functools.partial(body, rows, cols)
    return jax.shard_map(run, mesh=mesh, in_specs=(spec,) * 4, out_specs=(spec,) * 4, check_vma=False)
```

```python
import functools
import math

import jax
import jax.numpy as jnp
from jax import lax
from jax.experimental import pallas as pl
from jax.experimental.pallas import tpu as pltpu
from jax.sharding import PartitionSpec as P


STEPS = 2


inverse_width = 0.03125
grad_scale = 0.0625
descent_rate = 0.3


f32 = jnp.float32
bf16 = jnp.bfloat16
exp2_scale = inverse_width * math.log2(math.e)
step_scale = descent_rate * grad_scale
LAST = (((1,), (1,)), ((), ()))
FIRST = (((0,), (0,)), ((), ()))
VMEM_BUDGET = 40 << 20


def tile_terms(left_bf, left_panel, right_bf, right_panel):
    left_rows = left_bf.shape[0]
    block_rows = min(512, left_rows)
    block_count = left_rows // block_rows
    feature_width = left_bf.shape[1]
    right_wide = right_bf.astype(jnp.float32)
    right_norm = jnp.sum(right_wide * right_wide, axis=1)
    contract_last = (((1,), (1,)), ((), ()))

    def visit_block(carried, pieces):
        accumulated, column_sum = carried
        piece_feat, piece_panel = pieces
        piece_wide = piece_feat.astype(jnp.float32)
        left_norm = jnp.sum(piece_wide * piece_wide, axis=1)
        crossed = lax.dot_general(
            piece_feat, right_bf, contract_last, preferred_element_type=jnp.float32
        )
        distance = left_norm[:, None] + right_norm[None, :] - 2.0 * crossed
        kernel = jnp.exp(-inverse_width * distance).astype(jnp.bfloat16)
        weight = lax.dot_general(
            piece_panel, right_panel, contract_last, preferred_element_type=jnp.float32
        )
        product = (weight * kernel.astype(jnp.float32)).astype(jnp.bfloat16)
        product_wide = product.astype(jnp.float32)
        left_term = (
            jnp.dot(product, right_bf, preferred_element_type=jnp.float32)
            - jnp.sum(product_wide, axis=1)[:, None] * piece_wide
        )
        accumulated = accumulated + lax.dot_general(
            product, piece_feat, (((0,), (0,)), ((), ())), preferred_element_type=jnp.float32
        )
        column_sum = column_sum + jnp.sum(product_wide, axis=0)
        return ((accumulated, column_sum), left_term)

    initial = (
        jnp.zeros((right_bf.shape[0], feature_width), jnp.float32),
        jnp.zeros((right_bf.shape[0],), jnp.float32),
    )
    pieces = (
        left_bf.reshape(block_count, block_rows, feature_width),
        left_panel.reshape(block_count, block_rows, left_panel.shape[1]),
    )
    (accumulated, column_sum), left_terms = lax.scan(visit_block, initial, pieces)
    return (
        left_terms.reshape(left_rows, feature_width),
        accumulated - column_sum[:, None] * right_wide,
    )


def partitioned_body(left_points, right_points, left_cotangent, right_coefficient):
    left_panel = lax.all_gather(left_cotangent, "col", axis=0, tiled=True)
    right_panel = lax.all_gather(right_coefficient, "row", axis=0, tiled=True)
    left_own = left_points
    right_own = right_points
    left_grad = jnp.zeros_like(left_points)
    right_grad = jnp.zeros_like(right_points)
    for step_index in range(STEPS):
        left_bf = lax.all_gather(left_own.astype(jnp.bfloat16), "col", axis=0, tiled=True)
        right_bf = lax.all_gather(right_own.astype(jnp.bfloat16), "row", axis=0, tiled=True)
        left_term, right_term = tile_terms(left_bf, left_panel, right_bf, right_panel)
        if step_index + 1 < STEPS:
            left_step = (
                lax.psum_scatter(left_term, "col", scatter_dimension=0, tiled=True) * grad_scale
            )
            right_step = (
                lax.psum_scatter(right_term, "row", scatter_dimension=0, tiled=True) * grad_scale
            )
            left_own = left_own - descent_rate * left_step
            right_own = right_own - descent_rate * right_step
        else:
            left_grad = (
                lax.psum_scatter(left_term, "col", scatter_dimension=0, tiled=True) * grad_scale
            )
            right_grad = (
                lax.psum_scatter(right_term, "row", scatter_dimension=0, tiled=True) * grad_scale
            )
            left_own = left_own - descent_rate * left_grad
            right_own = right_own - descent_rate * right_grad
    return (left_own, right_own, left_grad, right_grad)


def squares(wide):
    square = wide * wide
    high = square.astype(bf16)
    return jnp.concatenate([high, (square - high.astype(f32)).astype(bf16)], axis=1)


def norm_row(feat):
    both = squares(feat.astype(f32))
    return lax.dot_general(jnp.ones((8, both.shape[1]), bf16), both, LAST, preferred_element_type=f32)


def norm_column(feat):
    both = squares(feat.astype(f32))
    return jnp.dot(both, jnp.ones((both.shape[1], feat.shape[1]), bf16), preferred_element_type=f32)


def with_ones(feat):
    return jnp.concatenate([feat, jnp.ones_like(feat)], axis=1)


def rows_of(ref, side, kind):
    blocks, both, width = ref.shape[1:]
    points = both // 2
    return ref[side, :, kind * points : (kind + 1) * points, :].reshape(blocks * points, width)


def ones_rows(blocks, sets, side):
    return jnp.concatenate([with_ones(rows_of(blocks[x], side, 0)) for x in sets], axis=0)


def products(blocks, lefts, rights, place, left_norm, right_norm, product):
    size, width = left_norm.shape[1:]
    for m, left in enumerate(lefts):
        feat, panel = rows_of(blocks[left], 0, 0), rows_of(blocks[left], 0, 1)
        norm = jnp.concatenate([left_norm[place(left)]] * (size // width), axis=1)
        for n, k in enumerate(rights):
            crossed = lax.dot_general(feat, rows_of(blocks[k, 0], 1, 0), LAST, preferred_element_type=f32)
            weight = lax.dot_general(panel, rows_of(blocks[k, 0], 1, 1), LAST, preferred_element_type=f32)
            kernel = jnp.exp2((2.0 * exp2_scale) * crossed - norm - right_norm[k, 0:1, :])
            product[m * size : (m + 1) * size, n * size : (n + 1) * size] = (weight * kernel).astype(bf16)


def stage_kernel(plan, sets, *refs):
    rects, new_left, new_right, fresh_left, fresh_right, first, keep = plan
    count = len(sets)
    blocks = dict(zip(sets, refs[:count]))
    outs = refs[count + (0 if first else 4) :]
    left_sum, right_sum, left_norm, right_norm = outs[:4]
    fresh_left, fresh_right = set(fresh_left), set(fresh_right)

    def place(left):
        return left[1] * (left_sum.shape[0] // 2) + left[0]

    for left in new_left:
        left_norm[place(left)] = exp2_scale * norm_column(rows_of(blocks[left], 0, 0))
    for k in new_right:
        right_norm[k] = exp2_scale * norm_row(rows_of(blocks[k, 0], 1, 0))
    for index, (lefts, rights) in enumerate(rects):
        product = outs[4 + keep.index(index)] if index in keep else outs[-1]
        products(blocks, lefts, rights, place, left_norm, right_norm, product)
        others = ones_rows(blocks, [(k, 0) for k in rights], 1)
        size = others.shape[0] // len(rights)
        for m, left in enumerate(lefts):
            term = jnp.dot(
                product[m * size : (m + 1) * size, : len(rights) * size], others, preferred_element_type=f32
            )
            if left in fresh_left:
                fresh_left.discard(left)
                left_sum[place(left)] = term
            else:
                left_sum[place(left)] += term
        if index in keep:
            continue
        others = ones_rows(blocks, lefts, 0)
        for n, k in enumerate(rights):
            term = lax.dot_general(
                product[: len(lefts) * size, n * size : (n + 1) * size], others, FIRST, preferred_element_type=f32
            )
            if k in fresh_right:
                fresh_right.discard(k)
                right_sum[k] = term
            else:
                right_sum[k] += term


def left_kernel(rows, points_left, left_sum, right_norm, *refs):
    every, (sent, base, own, product, left_norm) = refs[: 2 * rows], refs[2 * rows :]
    blocks = {(i % rows, i // rows): x for i, x in enumerate(every)}
    last = (rows - 1, 1)
    size, width = left_sum.shape[1], left_sum.shape[2] // 2
    rights = list(range(rows))
    left_norm[0] = exp2_scale * norm_column(rows_of(blocks[last], 0, 0))
    products(blocks, [last], rights, lambda _: 0, left_norm, right_norm, product)
    for index in range(2 * rows):
        if index < 2 * rows - 1:
            both = left_sum[index]
        else:
            both = jnp.dot(product[...], ones_rows(blocks, [(k, 0) for k in rights], 1), preferred_element_type=f32)
        wide = rows_of(every[index], 0, 0).astype(f32)
        change = step_scale * (both[:, :width] - both[:, width:] * wide)
        sent[index * size : (index + 1) * size, :] = change.astype(bf16)
        base[index * size : (index + 1) * size, :] = wide - change
        if index == 0:
            own[...] = points_left[...] - change[: own.shape[0], :]


def right_kernel(rows, summed, pieces, points_right, right_sum, *refs):
    kept, refs = refs[: len(pieces)], refs[len(pieces) :]
    every, (sent, norms, own) = refs[: 2 * rows], refs[2 * rows :]
    blocks = {(i % rows, i // rows): x for i, x in enumerate(every)}
    size, width = right_sum.shape[1], right_sum.shape[2] // 2
    for index in range(rows):
        terms = [right_sum[index]] if index in summed else []
        for (lefts, rights), product in zip(pieces, kept):
            if index in rights:
                n = rights.index(index)
                terms.append(
                    lax.dot_general(
                        product[:, n * size : (n + 1) * size],
                        ones_rows(blocks, lefts, 0),
                        FIRST,
                        preferred_element_type=f32,
                    )
                )
        both = sum(terms[1:], terms[0])
        wide = rows_of(every[index], 1, 0).astype(f32)
        change = step_scale * (both[:, :width] - both[:, width:] * wide)
        new = (wide - change).astype(bf16)
        sent[index * size : (index + 1) * size, :] = new
        norms[:, index * size : (index + 1) * size] = norm_row(new)
        if index == 0:
            own[...] = points_right[...] - change[: own.shape[0], :]


def own_weights_kernel(rows, sets, *refs):
    mine, every = refs[0], refs[1 : 1 + len(sets)]
    left_weight, right_weight = refs[-2:]
    points = left_weight.shape[0]
    size = left_weight.shape[1] // (2 * rows)
    for side, out in ((0, left_weight), (1, right_weight)):
        panel = mine[side, 0, points:, :]
        for (k, half), ref in zip(sets, every):
            index = half * rows + k
            out[:, index * size : (index + 1) * size] = lax.dot_general(
                panel, rows_of(ref, 1 - side, 1), LAST, preferred_element_type=f32
            )


def own_term(feat, weight, others, other_norm):
    crossed = lax.dot_general(feat, others, LAST, preferred_element_type=f32)
    wide = feat.astype(f32)
    norm = jnp.sum(wide * wide, axis=1, keepdims=True)
    kernel = jnp.exp2(exp2_scale * (2.0 * crossed - norm - other_norm))
    product = (weight * kernel).astype(bf16)
    total = jnp.sum(product.astype(f32), axis=1, keepdims=True)
    return jnp.dot(product, others, preferred_element_type=f32) - total * wide


def last_right_kernel(base, came, sent, sent_norm, own_right, own_left, right_weight, left_weight, *outs):
    new, grad, left_value, left_term = outs
    half, points = sent.shape[0], own_left.shape[0]
    left = own_left[...] - came[half : half + points, :].astype(f32)
    left_value[...] = left
    left_term[...] = own_term(left.astype(bf16), left_weight[:, :half], sent[...], sent_norm[0:1, :])
    others = [
        (base[:half, :] - came[half:, :].astype(f32)).astype(bf16),
        (base[half:, :] - came[:half, :].astype(f32)).astype(bf16),
    ]
    norm = jnp.concatenate([norm_row(x)[0:1, :] for x in others], axis=1)
    others = jnp.concatenate(others, axis=0)
    value = own_right[...]
    term = grad_scale * own_term(value.astype(bf16), right_weight[...], others, norm)
    grad[...] = term
    new[...] = value - descent_rate * term


def last_left_kernel(came, left_value, left_term, weight, right_new, right_grad, *refs):
    outs, (new, grad, sems) = refs[:4], refs[4:]
    copies = [
        pltpu.make_async_copy(x, out, sems.at[i])
        for i, (x, out) in enumerate(zip((right_new, right_grad, new, grad), (outs[1], outs[3], outs[0], outs[2])))
    ]
    copies[0].start()
    copies[1].start()
    half = came.shape[0]
    value = left_value[...]
    others = came[...]
    term = left_term[...] + own_term(value.astype(bf16), weight[:, half:], others, norm_row(others)[0:1, :])
    term = grad_scale * term
    grad[...] = term
    new[...] = value - descent_rate * term
    copies[2].start()
    copies[3].start()
    for copy in copies:
        copy.wait()


def pack_kernel(left, right, left_panel, right_panel, out, left_held, right_held, sems):
    points = left.shape[0]
    moves = ((left, left_held), (right, right_held), (left_panel, out.at[0, points:]), (right_panel, out.at[1, points:]))
    copies = [pltpu.make_async_copy(source, target, sems.at[i]) for i, (source, target) in enumerate(moves)]
    for copy in copies:
        copy.start()
    for copy in copies:
        copy.wait()
    out[0, :points, :] = left_held[...].astype(bf16)
    out[1, :points, :] = right_held[...].astype(bf16)


def call(kernel, inputs, outputs, scratch=(), aliases=None, flops=0, in_space=pltpu.VMEM, out_space=pltpu.VMEM, limit=VMEM_BUDGET):
    moved = sum(x.size * x.dtype.itemsize for x in (*inputs, *outputs))
    return pl.pallas_call(
        kernel,
        out_shape=tuple(outputs),
        in_specs=[pl.BlockSpec(memory_space=in_space)] * len(inputs),
        out_specs=(pl.BlockSpec(memory_space=out_space),) * len(outputs),
        scratch_shapes=list(scratch),
        input_output_aliases=aliases or {},
        cost_estimate=pl.CostEstimate(flops=flops, bytes_accessed=moved // 8, transcendentals=0),
        compiler_params=pltpu.CompilerParams(vmem_limit_bytes=limit),
    )(*inputs)


def replicated_body(rows, cols, left_points, right_points, left_cotangent, right_coefficient):
    points, width = left_points.shape
    pairs = cols // 2
    size = pairs * points
    shape = jax.ShapeDtypeStruct

    def along_col(x, k):
        return lax.ppermute(x, "col", [(i, (i + 2 * k) % cols) for i in range(cols)])

    def along_row(x, k):
        def target(i):
            return i ^ k if rows & (rows - 1) == 0 else (i + k) % rows

        return lax.ppermute(x, "row", [(i, target(i)) for i in range(rows)])

    def partner(x):
        return lax.ppermute(x, "col", [(i, i ^ 1) for i in range(cols)])

    own_shape = shape((points, width), f32)
    packed, left_held, right_held = call(
        pack_kernel,
        [pltpu.with_memory_space_constraint(x, pltpu.HBM) for x in (left_points, right_points, left_cotangent, right_coefficient)],
        [shape((2, 2 * points, width), bf16), own_shape, own_shape],
        [pltpu.SemaphoreType.DMA((4,))],
        in_space=pl.ANY,
    )
    line = [along_col(packed, k) for k in range(1, pairs)]
    across = jnp.concatenate(line, axis=1)
    direct = [packed] + [along_row(packed, k) for k in range(1, rows)]
    rest = [across] + [along_row(across, k) for k in range(1, rows - 1)]
    own = jnp.concatenate([x for k, x in enumerate(line, 1) if k not in (1,)], axis=1)
    own = jnp.split(along_row(own, rows - 1), pairs - 1 - len((1,)), axis=1)
    parts = [along_col(direct[-1], k) if k in (1,) else own.pop(0) for k in range(1, pairs)]
    rest.append(jnp.concatenate(parts, axis=1))
    blocks = {}
    for k in range(rows):
        near = jnp.concatenate([direct[k], rest[k]], axis=1)
        blocks[k, 0] = near.reshape(2, pairs, 2 * points, width)
        blocks[k, 1] = partner(near).reshape(2, pairs, 2 * points, width)

    state = (
        shape((2 * rows, size, 2 * width), f32),
        shape((rows, size, 2 * width), f32),
        shape((2 * rows, size, width), f32),
        shape((rows, 8, size), f32),
    )
    values = None
    seen_left, seen_right = set(), set()

    def stage(rects, new_left, new_right, keep=()):
        nonlocal values
        sets = sorted({x for lefts, _ in rects for x in lefts} | {(k, 0) for _, rights in rects for k in rights})
        lefts = {x for part, _ in rects for x in part}
        rights = {k for _, part in rects for k in part}
        plan = (rects, new_left, new_right, lefts - seen_left, rights - seen_right, values is None, keep)
        seen_left.update(lefts)
        seen_right.update(k for i, (_, part) in enumerate(rects) if i not in keep for k in part)
        places = [(len(a) * size, len(b) * size) for a, b in rects]
        inner = [x for i, x in enumerate(places) if i not in keep]
        inputs = [blocks[x] for x in sets] + list(values or ())
        values = call(
            functools.partial(stage_kernel, plan, sets),
            inputs,
            state + tuple(shape(places[i], bf16) for i in keep),
            [pltpu.VMEM(tuple(max(x) for x in zip(*inner)), bf16)] if inner else [],
            aliases={len(sets) + i: i for i in range(4)} if values else None,
            flops=sum(len(a) * len(b) for a, b in rects) * 12 * size * size * width,
        )

    held = ()

    def weights(sets):
        return call(
            functools.partial(own_weights_kernel, rows, sets),
            [blocks[0, 0]] + [blocks[x] for x in sets] + list(held),
            [shape((points, 2 * rows * size), f32)] * 2,
            aliases={1 + len(sets) + i: i for i in range(2)} if held else None,
        )

    waiting = []
    for k in range(rows):
        if k == rows - 1:
            held = weights([(i, half) for half in (0, 1) for i in range(k)])
        old = [(i, half) for half in (0, 1) for i in range(k) if (i, half) in seen_left]
        rects = ([(old, [k])] if old else []) + [([(k, 0)], list(range(k + 1)))]
        stage(rects, [(k, 0)], [k], keep=(0,) if k == rows - 1 else ())
        if k == rows - 1:
            kept, values, pieces = values[4:], values[:4], rects[:1]
        waiting.append((k, 1))
        if k != 1 and k != rows - 1:
            stage([(waiting, list(range(k + 1)))], waiting, [])
            waiting = []
    if waiting[:-1]:
        more = [(waiting[:-1], list(range(rows)))]
        stage(more, waiting[:-1], [], keep=(0,))
        kept, values, pieces = [*kept, *values[4:]], values[:4], pieces + more
    left_sum, right_sum, _, right_norm = values
    near = [blocks[k, 0] for k in range(rows)]
    every = near + [blocks[k, 1] for k in range(rows)]
    left_sent, left_base, left_own, product = call(
        functools.partial(left_kernel, rows),
        [left_held, left_sum, right_norm] + every,
        [
            shape((2 * rows * size, width), bf16),
            shape((2 * rows * size, width), f32),
            own_shape,
            shape((size, rows * size), bf16),
        ],
        [pltpu.VMEM((1, size, width), f32)],
    )
    left_came = partner(left_sent)
    pieces = pieces + [([(rows - 1, 1)], list(range(rows)))]
    right_sent, right_row_norm, right_own = call(
        functools.partial(right_kernel, rows, seen_right, pieces),
        [right_held, right_sum, *kept, product] + every,
        [shape((rows * size, width), bf16), shape((8, rows * size), f32), own_shape],
    )
    right_came = partner(right_sent)
    left_weight, right_weight = weights([(rows - 1, 0), (rows - 1, 1)])
    right_new, right_grad, left_value, left_term = call(
        last_right_kernel,
        [left_base, left_came, right_sent, right_row_norm, right_own, left_own, right_weight, left_weight],
        [own_shape] * 4,
    )
    return call(
        last_left_kernel,
        [right_came, left_value, left_term, left_weight, right_new, right_grad],
        [own_shape] * 4,
        [pltpu.VMEM((points, width), f32)] * 2 + [pltpu.SemaphoreType.DMA((4,))],
        out_space=pltpu.HBM,
    )


def replicated(rows, cols, shapes):
    points, width = shapes[0]
    total = rows * cols * points
    held = total * total + 24 * total * width
    size = cols // 2 * points
    even = cols % 2 == 0 and width % 128 == 0 and size % width == 0 and rows > 2 and cols > 2
    return STEPS == 2 and even and len(set(shapes)) == 1 and held <= VMEM_BUDGET // 2


def body(rows, cols, *arrays):
    if replicated(rows, cols, [x.shape for x in arrays]):
        return replicated_body(rows, cols, *arrays)
    return partitioned_body(*arrays)


def solution(mesh):
    spec = P(("row", "col"), None)
    rows, cols = mesh.shape["row"], mesh.shape["col"]
    run = functools.partial(body, rows, cols)
    return jax.shard_map(run, mesh=mesh, in_specs=(spec,) * 4, out_specs=(spec,) * 4, check_vma=False)
```
